32 devices in a mesh: feed: 8 (over z, x), chan: 2 (over y), tm: 2 (over core).
Axes of the slice: x: 2, y: 2, z: 4, core: 2. Of those that a mesh axis runs over, the one named last changes fastest.
Arguments:
- voltages: bfloat16 [2, 512, 8, 2, 4096], P(None, 'tm', 'chan', None, 'feed'), may hold values from -6 to 6
- beam_refs: bfloat16 [2, 2, 8, 32, 8, 2, 32, 512], P(None, 'tm', 'feed', None, 'chan'), may hold values from -3 to 3
- beam_weight: float32 [32, 512], replicated, may hold values from 0.25 to 4
- delays: float32 [2, 4096], P(None, 'feed'), may hold values from -3 to 3
- band_phase: float32 [2, 16], replicated, may hold values from -4 to 4
- rfi_flags: int32 [512, 8], P('tm', 'chan'), may hold values 0 or 1
- grid_rows: int32 [256], replicated, may hold values from 0 to 255, each once
Outputs:
- delay_grad: float32 [2, 4096], P(None, 'feed')
- band_grad: float32 [2, 16], replicated
The draws below stay inside these ranges and needn't reach their ends.
Inputs may be any that keep to these rules, and one draw needn't show every extreme that they name: `grid_rows`: every row 0 to 255 is taken by exactly one feed position, the same for every cylinder.
All inputs are finite; a program needn't handle non-finite values. No bound on the sum of `rfi_flags` on one device may be relied on, other than what follows from the above.
Results may differ from the reference program's by a relative error of at most 0.017.
Values may be sent and summed in bfloat16 or wider, within the bound.
No kernel may reach another device: no remote copies, remote signals or barrier semaphores. Data moves between devices by JAX's collectives and lax.ppermute only.
A program may use at most 128 MiB of HBM per device.

```python
import math
import jax
import jax.numpy as jnp
from jax import lax

CYL = 16
NSF = 256
EWB = 32
NSB = 512
POL = 2
BANDS = 16
FEEDS = 4096
TIMES = 512
CHANS = 8
TIME_GROUPS = 2
SUB_GROUPS = 8
SUB_TIMES = 32


def with_ends(array, rng, least, high):
    dims = array.shape
    spot = [jax.random.randint(jax.random.fold_in(rng, axis), (), 0, dims[axis]) for axis in range(len(dims))]
    array = array.at[tuple(spot)].set(least)
    longest = dims.index(max(dims))
    spot[longest] = (spot[longest] + 1) % dims[longest]
    return array.at[tuple(spot)].set(high)


def shard_levels(stream_key, shape, shards, least, largest):
    def one(dim, parts):
        heights = jax.random.uniform(jax.random.fold_in(jax.random.fold_in(stream_key, 6), dim), (parts,), jnp.float32, least / len(shards), largest / len(shards))
        return jnp.repeat(jnp.exp(heights), shape[dim] // parts).reshape((-1,) + (1,) * (len(shape) - dim - 1))

    level = one(*shards[0])
    for cut in shards[1:]:
        level = level * one(*cut)
    return level


def centred(rng, dims, scale, limit, shards=(), kind=jnp.bfloat16):
    drawn = jax.random.normal(rng, dims, jnp.float32) * scale
    if len(shards) > 0:
        drawn = shard_levels(rng, dims, shards, -0.22, 0.18) * drawn
    return jnp.clip(drawn, min=-limit, max=limit).astype(kind)


def setup_inputs(seed: int = 0) -> dict:
    keys = jax.random.split(jax.random.key(seed), 8)
    voltages = centred(keys[0], (2, TIMES, CHANS, POL, FEEDS), 1.0, 6.0, ((1, 2), (2, 2), (4, 8)))
    beam_refs = centred(keys[1], (2, TIME_GROUPS, SUB_GROUPS, SUB_TIMES, CHANS, POL, EWB, NSB), 0.5, 3.0, ((1, 2), (2, 8), (4, 2)))
    beam_weight = jnp.clip(jnp.exp(jax.random.uniform(keys[2], (EWB, NSB), jnp.float32, math.log(0.25), math.log(4.0))), 0.25, 4.0)
    delays = jnp.clip(jax.random.uniform(keys[3], (POL, FEEDS), jnp.float32, -3.0, 3.0) * shard_levels(keys[3], (POL, FEEDS), ((1, 8),), -0.4, 0.0), -3.0, 3.0)
    band_phase = centred(keys[4], (POL, BANDS), 1.0, 4.0, (), jnp.float32)
    rfi_flags = with_ends((jax.random.randint(keys[5], (TIMES, CHANS), 0, 8) < 1).astype(jnp.int32), jax.random.fold_in(keys[5], 1), 0, 1)
    grid_rows = jax.random.permutation(keys[6], NSF).astype(jnp.int32)
    return dict(voltages=voltages, beam_refs=beam_refs, beam_weight=beam_weight, delays=delays, band_phase=band_phase, rfi_flags=rfi_flags, grid_rows=grid_rows)


full_turn = 2.0 * math.pi

def rounded(value):
    return lax.optimization_barrier(value.astype(jnp.bfloat16)).astype(jnp.float32)

def product(form, left, right):
    return jnp.einsum(form, left, right, precision=lax.Precision.HIGHEST)

def dft_parts(grid_rows):
    cyl_index = jnp.arange(CYL, dtype=jnp.int32)
    east_index = jnp.arange(EWB, dtype=jnp.int32)
    east_angle = full_turn / EWB * (east_index[:, None] * cyl_index[None, :] % EWB).astype(jnp.float32)
    north_index = jnp.arange(NSB, dtype=jnp.int32)
    north_angle = full_turn / NSB * (north_index[:, None] * grid_rows.astype(jnp.int32)[None, :] % NSB).astype(jnp.float32)
    east_real = (jnp.cos(east_angle) / math.sqrt(EWB)).astype(jnp.bfloat16)
    east_imag = (-jnp.sin(east_angle) / math.sqrt(EWB)).astype(jnp.bfloat16)
    north_real = (jnp.cos(north_angle) / math.sqrt(NSB)).astype(jnp.bfloat16)
    north_imag = (-jnp.sin(north_angle) / math.sqrt(NSB)).astype(jnp.bfloat16)
    return (east_real, east_imag, north_real, north_imag)

def band_basis(chan_index, chans_total):
    term_index = jnp.arange(BANDS).astype(jnp.float32)
    return math.sqrt(2.0 / chans_total) * jnp.cos(math.pi * (chan_index[:, None] + 0.5) * term_index[None, :] / chans_total)

def reference(voltages, beam_refs, beam_weight, delays, band_phase, rfi_flags, grid_rows):
    tables = dft_parts(grid_rows)
    east_real = tables[0].astype(jnp.float32)
    east_imag = tables[1].astype(jnp.float32)
    north_real = tables[2].astype(jnp.float32)
    north_imag = tables[3].astype(jnp.float32)
    chan_index = jnp.arange(CHANS).astype(jnp.float32)
    frequency = 0.4 + 0.4 * (chan_index + 0.5) / CHANS
    basis = band_basis(chan_index, CHANS)
    offset = jnp.dot(band_phase, basis.T, precision=lax.Precision.HIGHEST)
    phases = full_turn * frequency[None, :, None] * delays[:, None, :] + offset[:, :, None]
    gain_real = jnp.transpose(jnp.cos(phases), (1, 0, 2))[None]
    gain_imag = jnp.transpose(-jnp.sin(phases), (1, 0, 2))[None]
    ref_field = beam_refs.reshape(2, TIMES, CHANS, POL, EWB, NSB)
    time_block = 8

    def advance(block_index, totals):
        time_start = (block_index * time_block).astype(jnp.int32)
        volt_block = lax.dynamic_slice_in_dim(voltages, time_start, time_block, 1).astype(jnp.float32)
        ref_block = lax.dynamic_slice_in_dim(ref_field, time_start, time_block, 1).astype(jnp.float32)
        flag_block = lax.dynamic_slice_in_dim(rfi_flags, time_start, time_block, 0)
        sky_real = rounded(gain_real * volt_block[0] - gain_imag * volt_block[1])
        sky_imag = rounded(gain_real * volt_block[1] + gain_imag * volt_block[0])
        grid_shape = (time_block, CHANS, POL, NSF, CYL)
        grid_real = sky_real.reshape(grid_shape)
        grid_imag = sky_imag.reshape(grid_shape)
        east_re = rounded(product('tfpnc,ec->tfpen', grid_real, east_real) - product('tfpnc,ec->tfpen', grid_imag, east_imag))
        east_im = rounded(product('tfpnc,ec->tfpen', grid_real, east_imag) + product('tfpnc,ec->tfpen', grid_imag, east_real))
        beam_re = product('tfpen,mn->tfpem', east_re, north_real) - product('tfpen,mn->tfpem', east_im, north_imag)
        beam_im = product('tfpen,mn->tfpem', east_re, north_imag) + product('tfpen,mn->tfpem', east_im, north_real)
        keep_weight = ((1 - flag_block).astype(jnp.float32) / TIMES)[:, :, None, None, None]
        resid_re = rounded(keep_weight * beam_weight * (beam_re - ref_block[0]))
        resid_im = rounded(keep_weight * beam_weight * (beam_im - ref_block[1]))
        back_re = rounded(product('tfpem,mn->tfpen', resid_re, north_real) + product('tfpem,mn->tfpen', resid_im, north_imag))
        back_im = rounded(product('tfpem,mn->tfpen', resid_im, north_real) - product('tfpem,mn->tfpen', resid_re, north_imag))
        field_re = rounded(product('tfpen,ec->tfpnc', back_re, east_real) + product('tfpen,ec->tfpnc', back_im, east_imag))
        field_im = rounded(product('tfpen,ec->tfpnc', back_im, east_real) - product('tfpen,ec->tfpnc', back_re, east_imag))
        flat_shape = (time_block, CHANS, POL, CYL * NSF)
        torque = field_re.reshape(flat_shape) * sky_imag - field_im.reshape(flat_shape) * sky_real
        delay_total = totals[0] + product('tfpj,f->pj', torque, full_turn * frequency)
        chan_total = totals[1] + lax.optimization_barrier(jnp.sum(torque, axis=(0, 3))).T
        return (delay_total, chan_total)
    start_totals = (jnp.zeros((POL, CYL * NSF), jnp.float32), jnp.zeros((POL, CHANS), jnp.float32))
    delay_total, chan_total = lax.fori_loop(0, TIMES // time_block, advance, start_totals)
    band_grad = jnp.dot(chan_total, basis, precision=lax.Precision.HIGHEST)
    return (delay_total, band_grad)
```

```python
import math

import jax
import jax.numpy as jnp
import numpy as np
from jax import lax
from jax.experimental import pallas as pl
from jax.experimental.pallas import tpu as pltpu
from jax.sharding import PartitionSpec as P

CYL = 16
NSF = 256
EWB = 32
NSB = 512
BANDS = 16
ROWS = 8
LANES = 128


full_turn = 2.0 * math.pi


def east_tables():
    angle = np.float32(full_turn / EWB) * (
        np.arange(EWB)[:, None] * np.arange(CYL)[None, :] % EWB
    ).astype(np.float32)
    real = np.cos(angle) / np.float32(math.sqrt(EWB))
    imag = -np.sin(angle) / np.float32(math.sqrt(EWB))
    parts = np.array([[real, -imag], [imag, real]], np.float32)
    same = np.eye(ROWS, dtype=np.float32)
    forward = np.einsum("abec,rs->arebcs", parts, same)
    forward = forward.reshape(2 * ROWS * EWB, 2 * CYL * ROWS)
    return jnp.asarray(forward, jnp.bfloat16), jnp.asarray(forward.T, jnp.bfloat16)


def cylinder_major(width):
    lane = np.arange(width)
    target = (lane % CYL) * (width // CYL) + lane // CYL
    matrix = np.zeros((width, width), np.float32)
    matrix[lane, target] = 1.0
    return jnp.asarray(matrix, jnp.bfloat16)


def north_table(rows):
    north_index = jnp.arange(NSB, dtype=jnp.int32)
    angle = (
        full_turn / NSB * (rows[:, None] * north_index[None, :] % NSB).astype(jnp.float32)
    )
    real = (jnp.cos(angle) / math.sqrt(NSB)).astype(jnp.bfloat16)
    imag = (-jnp.sin(angle) / math.sqrt(NSB)).astype(jnp.bfloat16)
    return jnp.concatenate(
        [jnp.concatenate([real, imag], 1), jnp.concatenate([-imag, real], 1)], 0
    )


def band_basis(chan_index, chans_total):
    term_index = jnp.arange(BANDS).astype(jnp.float32)
    return math.sqrt(2.0 / chans_total) * jnp.cos(
        math.pi * (chan_index[:, None] + 0.5) * term_index[None, :] / chans_total
    )


def beam_kernel(peers, width, *refs):
    blocks = refs[:peers]
    (ref_beams, keep, weight, order, east_fwd, east_adj, north_fwd, north_adj) = refs[
        peers : peers + 8
    ]
    out = refs[peers + 8]
    span = width // CYL
    stacked = jnp.concatenate(
        [blocks[k][part, 0, 0].astype(jnp.float32) for part in range(2) for k in range(peers)], 0
    ).astype(jnp.bfloat16)
    ordered = jnp.dot(stacked, order[...], preferred_element_type=jnp.float32)
    lane = lax.broadcasted_iota(jnp.int32, (ROWS, LANES), 1) // span
    per_tile = LANES // span
    pieces = []
    for part in range(2):
        for c in range(CYL):
            tile, start = divmod(c * span, LANES)
            halves = []
            for half in range(NSF // LANES):
                value = None
                for slot in range(per_tile):
                    row = (part * peers + half * per_tile + slot) * ROWS
                    piece = ordered[row : row + ROWS, tile * LANES : (tile + 1) * LANES]
                    shift = (slot * span - start) % LANES
                    if shift:
                        piece = pltpu.roll(piece, shift, 1)
                    value = piece if value is None else jnp.where(lane == slot, piece, value)
                halves.append(value)
            pieces.append(jnp.concatenate(halves, 1))
    sky = jnp.concatenate(pieces, 0)
    east = jnp.dot(east_fwd[...], sky.astype(jnp.bfloat16), preferred_element_type=jnp.float32)
    east = east.astype(jnp.bfloat16)
    half = ROWS * EWB
    east = jnp.concatenate([east[:half], east[half:]], 1)
    beams = jnp.dot(east, north_fwd[...], preferred_element_type=jnp.float32)
    beams = beams.reshape(ROWS, EWB, 2 * NSB)
    residual = jnp.concatenate(
        [
            (
                (beams[:, :, part * NSB : (part + 1) * NSB] - ref_beams[part, :, 0, 0].astype(jnp.float32))
                * weight[...][None]
            ).astype(jnp.bfloat16)
            for part in range(2)
        ],
        2,
    ).reshape(half, 2 * NSB)
    back = jnp.dot(residual, north_adj[...], preferred_element_type=jnp.float32)
    back = back.astype(jnp.bfloat16)
    back = jnp.concatenate([back[:, :NSF], back[:, NSF:]], 0)
    field = jnp.dot(east_adj[...], back, preferred_element_type=jnp.float32)
    rows = CYL * ROWS
    torque = field[:rows] * sky[rows:] - field[rows:] * sky[:rows]
    torque = torque.reshape(CYL, ROWS, NSF) * keep[0][None, :, :1]
    out[0, 0] = jnp.sum(torque, 1)


def chunk_torque(blocks, ref_beams, keep, weight, tables, chunk):
    peers = len(blocks)
    width = blocks[0].shape[-1]
    chans, pols = blocks[0].shape[1:3]
    whole = lambda shape: pl.BlockSpec(
        shape, lambda f, p: (0,) * len(shape), pipeline_mode=pl.Buffered(1)
    )
    return pl.pallas_call(
        lambda *refs: beam_kernel(peers, width, *refs),
        grid=(chans, pols),
        in_specs=[pl.BlockSpec((2, 1, 1, ROWS, width), lambda f, p: (0, f, p, 0, 0))] * peers
        + [
            pl.BlockSpec((2, ROWS, 1, 1, EWB, NSB), lambda f, p: (0, chunk, f, p, 0, 0)),
            pl.BlockSpec((1, ROWS, LANES), lambda f, p: (f, chunk, 0)),
            whole(weight.shape),
        ]
        + [whole(t.shape) for t in tables],
        out_specs=pl.BlockSpec((1, 1, CYL, NSF), lambda f, p: (f, p, 0, 0)),
        out_shape=jax.ShapeDtypeStruct((chans, pols, CYL, NSF), jnp.float32),
        compiler_params=pltpu.CompilerParams(vmem_limit_bytes=48 << 20),
        name="beams",
    )(*blocks, ref_beams, keep, weight, *tables)


def shards(voltages, beam_refs, beam_weight, delays, band_phase, rfi_flags, grid_rows):
    _, local_times, local_chans, pol_count, width = voltages.shape
    peers = lax.axis_size("feed")
    me = lax.axis_index("feed")
    others = lax.axis_size("chan") * lax.axis_size("tm")
    times_total = local_times * lax.axis_size("tm")
    chans_total = local_chans * lax.axis_size("chan")
    block_times = local_times // peers
    chunks = block_times // ROWS
    chan_index = (
        lax.axis_index("chan") * local_chans + jnp.arange(local_chans, dtype=jnp.int32)
    ).astype(jnp.float32)
    frequency = 0.4 + 0.4 * (chan_index + 0.5) / chans_total
    basis = band_basis(chan_index, chans_total)
    offset = jnp.dot(band_phase, basis.T, precision=lax.Precision.HIGHEST)
    phases = full_turn * frequency[None, :, None] * delays[:, None, :] + offset[:, :, None]
    gain_real = jnp.transpose(jnp.cos(phases), (1, 0, 2))[:, :, None]
    gain_imag = jnp.transpose(-jnp.sin(phases), (1, 0, 2))[:, :, None]

    def gained(chunk, partner):
        start = (me ^ partner) * block_times + chunk * ROWS
        block = lax.dynamic_slice_in_dim(voltages, start, ROWS, 1)
        block = jnp.transpose(block, (0, 2, 3, 1, 4)).astype(jnp.float32)
        return jnp.stack(
            [
                gain_real * block[0] - gain_imag * block[1],
                gain_real * block[1] + gain_imag * block[0],
            ]
        ).astype(jnp.bfloat16)

    order = list(range(peers // 2, peers)) + list(range(1, peers // 2))
    arrived = []
    for chunk in range(chunks):
        blocks = [None] * peers
        for partner in order:
            pairs = [(i, i ^ partner) for i in range(peers)]
            blocks[partner] = lax.ppermute(gained(chunk, partner), "feed", pairs)
        blocks[0] = gained(chunk, 0)
        arrived.append(blocks)

    rows = grid_rows.reshape(peers, -1)[me ^ jnp.arange(peers)].reshape(-1)
    north_fwd = north_table(rows)
    east_fwd, east_adj = east_tables()
    tables = (cylinder_major(width), east_fwd, east_adj, north_fwd, north_fwd.T)
    flags = lax.dynamic_slice_in_dim(rfi_flags, me * block_times, block_times, 0)
    keep = (1 - flags).astype(jnp.float32).T
    keep = jnp.broadcast_to(keep[:, :, None], (local_chans, block_times, LANES))
    ref_beams = beam_refs.reshape(2, block_times, local_chans, pol_count, EWB, NSB)
    torque = 0.0
    for chunk in range(chunks):
        torque += chunk_torque(arrived[chunk], ref_beams, keep, beam_weight, tables, chunk)
    torque = torque / times_total
    delay_part = jnp.sum(torque * (full_turn * frequency)[:, None, None, None], 0)
    chan_part = jnp.sum(torque, axis=(2, 3))
    band_part = jnp.sum(chan_part[:, :, None] * basis[:, None, :], 0)
    span = width // CYL
    delay_part = delay_part.reshape(pol_count, CYL, peers, span)
    delay_part = jnp.transpose(delay_part, (2, 0, 3, 1)).reshape(peers, -1)
    delay_part = delay_part[me ^ jnp.arange(peers)]
    slots = jnp.concatenate(
        [delay_part, jnp.broadcast_to(band_part.reshape(1, -1), (peers, band_part.size))], 1
    )
    slots = jnp.broadcast_to(slots[:, None], (peers, others, slots.shape[1]))
    slots = slots.reshape(peers * others, -1)
    total = jnp.sum(lax.all_to_all(slots, ("feed", "chan", "tm"), 0, 0, tiled=True), 0)
    cut = pol_count * width
    return total[:cut].reshape(pol_count, width), total[cut:].reshape(pol_count, BANDS)


def solution(mesh):
    in_specs = (
        P(None, "tm", "chan", None, "feed"),
        P(None, "tm", "feed", None, "chan", None, None, None),
        P(),
        P(None, "feed"),
        P(),
        P("tm", "chan"),
        P(),
    )
    out_specs = (P(None, "feed"), P())
    return jax.shard_map(shards, mesh=mesh, in_specs=in_specs, out_specs=out_specs, check_vma=False)
```

```python
import math

import jax
import jax.numpy as jnp
import numpy as np
from jax import lax
from jax.experimental import pallas as pl
from jax.experimental.pallas import tpu as pltpu
from jax.sharding import PartitionSpec as P

CYL = 16
NSF = 256
EWB = 32
NSB = 512
BANDS = 16
ROWS = 8
GROUPS = 4
LANES = 128


full_turn = 2.0 * math.pi


def east_tables():
    angle = np.float32(full_turn / EWB) * (
        np.arange(EWB)[:, None] * np.arange(CYL)[None, :] % EWB
    ).astype(np.float32)
    real = np.cos(angle) / np.float32(math.sqrt(EWB))
    imag = -np.sin(angle) / np.float32(math.sqrt(EWB))
    parts = np.array([[real, -imag], [imag, real]], np.float32)
    same = np.eye(ROWS, dtype=np.float32)
    forward = np.einsum("abec,rs->arebcs", parts, same)
    forward = forward.reshape(2 * ROWS * EWB, 2 * CYL * ROWS)
    return jnp.asarray(forward, jnp.bfloat16), jnp.asarray(forward.T, jnp.bfloat16)


def north_table(rows):
    north_index = jnp.arange(NSB, dtype=jnp.int32)
    angle = (
        full_turn / NSB * (rows[:, None] * north_index[None, :] % NSB).astype(jnp.float32)
    )
    real = (jnp.cos(angle) / math.sqrt(NSB)).astype(jnp.bfloat16)
    imag = (-jnp.sin(angle) / math.sqrt(NSB)).astype(jnp.bfloat16)
    return jnp.concatenate(
        [jnp.concatenate([real, imag], 1), jnp.concatenate([-imag, real], 1)], 0
    )


def band_basis(chan_index, chans_total):
    term_index = jnp.arange(BANDS).astype(jnp.float32)
    return math.sqrt(2.0 / chans_total) * jnp.cos(
        math.pi * (chan_index[:, None] + 0.5) * term_index[None, :] / chans_total
    )


def sky_kernel(partners, cuts, span, chan_start, chans_total, volts, delay_ref, band_ref, *refs):
    outs, (delays, band_phase, held, order, small, arrived) = refs[:-6], refs[-6:]
    _, _, times, chans, pols, width = held.shape
    me = lax.axis_index("feed")
    first_chan = lax.axis_index("chan") * volts.shape[2] + chan_start
    tables = [
        pltpu.make_async_copy(delay_ref, delays, small.at[0]),
        pltpu.make_async_copy(band_ref, band_phase, small.at[1]),
    ]
    for copy in tables:
        copy.start()
    copies = [
        pltpu.make_async_copy(
            volts.at[:, pl.ds((me ^ partner) * times, times), pl.ds(chan_start, chans)],
            held.at[index],
            arrived.at[index],
        )
        for index, partner in enumerate(partners)
    ]
    for copy in copies:
        copy.start()
    row = lax.broadcasted_iota(jnp.int32, (width, width), 0)
    column = lax.broadcasted_iota(jnp.int32, (width, width), 1)
    target = (row % CYL) * span + row // CYL
    order[...] = jnp.where(target == column, 1.0, 0.0).astype(jnp.bfloat16)
    term = lax.broadcasted_iota(jnp.int32, (1, BANDS), 1).astype(jnp.float32)
    for copy in tables:
        copy.wait()
    phases = []
    for chan in range(chans):
        place = (first_chan + chan).astype(jnp.float32)
        frequency = 0.4 + 0.4 * (place + 0.5) / chans_total
        basis = math.sqrt(2.0 / chans_total) * jnp.cos(
            math.pi * (place + 0.5) * term / chans_total
        )
        offset = jnp.sum(band_phase[...] * basis, 1, keepdims=True)
        phases.append(full_turn * frequency * delays[...] + offset)
    phases = jnp.concatenate(phases, 0)
    cosine, sine = jnp.cos(phases), -jnp.sin(phases)
    for index, partner in enumerate(partners):
        copies[index].wait()
        for chan in range(chans):
            block = held[index, :, :, chan].astype(jnp.float32)
            for pol in range(pols):
                unit = chan * pols + pol
                real, imag = block[0, :, pol], block[1, :, pol]
                gr, gi = cosine[unit : unit + 1], sine[unit : unit + 1]
                both = jnp.concatenate([gr * real - gi * imag, gr * imag + gi * real], 0)
                both = jnp.dot(
                    both.astype(jnp.bfloat16), order[...], preferred_element_type=jnp.float32
                )
                shift = partner * span % LANES
                if shift:
                    both = jnp.concatenate(
                        [
                            pltpu.roll(both[:, at : at + LANES], shift, 1)
                            for at in range(0, width, LANES)
                        ],
                        1,
                    )
                both = both.astype(jnp.bfloat16)
                piece = sum(unit >= cut for cut in cuts[1:-1])
                out = outs[index * (len(cuts) - 1) + piece]
                out[0, unit - cuts[piece]] = both[:times]
                out[1, unit - cuts[piece]] = both[times:]


def sky_blocks(voltages, delays, band_phase, peers, partners, part, cuts, chans_total):
    _, times, chans, pols, width = voltages.shape
    block = times // peers
    half = chans // 2
    outs = [
        jax.ShapeDtypeStruct((2, high - low, block, width), jnp.bfloat16)
        for _ in partners
        for low, high in zip(cuts[:-1], cuts[1:])
    ]
    result = pl.pallas_call(
        lambda *refs: sky_kernel(partners, cuts, width // CYL, part * half, chans_total, *refs),
        in_specs=[pl.BlockSpec(memory_space=pl.ANY)] * 3,
        out_specs=[pl.BlockSpec(memory_space=pltpu.VMEM)] * len(outs),
        scratch_shapes=[
            pltpu.VMEM(delays.shape, delays.dtype),
            pltpu.VMEM(band_phase.shape, band_phase.dtype),
            pltpu.VMEM((len(partners), 2, block, half, pols, width), jnp.bfloat16),
            pltpu.VMEM((width, width), jnp.bfloat16),
            pltpu.SemaphoreType.DMA((2,)),
            pltpu.SemaphoreType.DMA((len(partners),)),
        ],
        out_shape=outs,
        compiler_params=pltpu.CompilerParams(vmem_limit_bytes=48 << 20),
        name="sky",
    )(voltages, delays, band_phase)
    pieces = len(cuts) - 1
    return [result[i * pieces : (i + 1) * pieces] for i in range(len(partners))]


def group_torque(group, blocks, ref_beams, keep, weight, east_fwd, east_adj, north_fwd, north_adj):
    peers, width = len(blocks), blocks[0].shape[-1]
    span = width // CYL
    per_tile = LANES // span
    times = slice(group * ROWS, (group + 1) * ROWS)
    lane = lax.broadcasted_iota(jnp.int32, (ROWS, LANES), 1) // span
    pieces = []
    for part in range(2):
        loaded = [blocks[k][part, 0, times].astype(jnp.float32) for k in range(peers)]
        for c in range(CYL):
            tile, turn = divmod(c, per_tile)
            at = tile * LANES
            for half in range(NSF // LANES):
                value = None
                for slot in range(per_tile):
                    piece = loaded[half * per_tile + slot][:, at : at + LANES]
                    spot = (turn + slot) % per_tile
                    value = piece if value is None else jnp.where(lane == spot, piece, value)
                if turn:
                    value = pltpu.roll(value, LANES - turn * span, 1)
                pieces.append(value)
    sky = jnp.concatenate(
        [jnp.concatenate(pieces[i : i + 2], 1) for i in range(0, len(pieces), 2)], 0
    )
    east = jnp.dot(east_fwd[...], sky.astype(jnp.bfloat16), preferred_element_type=jnp.float32)
    east = east.astype(jnp.bfloat16)
    half = ROWS * EWB
    east = jnp.concatenate([east[:half], east[half:]], 1)
    beams = jnp.dot(east, north_fwd[...], preferred_element_type=jnp.float32)
    beams = beams.reshape(ROWS, EWB, 2 * NSB)
    residual = jnp.concatenate(
        [
            (
                (beams[:, :, part * NSB : (part + 1) * NSB] - ref_beams[part, times, 0, 0].astype(jnp.float32))
                * weight[...][None]
            ).astype(jnp.bfloat16)
            for part in range(2)
        ],
        2,
    ).reshape(half, 2 * NSB)
    back = jnp.dot(residual, north_adj[...], preferred_element_type=jnp.float32)
    back = back.astype(jnp.bfloat16)
    back = jnp.concatenate([back[:, :NSF], back[:, NSF:]], 0)
    field = jnp.dot(east_adj[...], back, preferred_element_type=jnp.float32)
    rows = CYL * ROWS
    torque = field[:rows] * sky[rows:] - field[rows:] * sky[:rows]
    torque = torque.reshape(CYL, ROWS, NSF) * keep[0, times][None, :, :1]
    return jnp.sum(torque, 1)


def beam_kernel(peers, groups, low, *refs):
    ref_beams, keep, weight, scales = refs[peers : peers + 4]
    before, out = refs[peers + 8 : -2], refs[-2:]
    torque = sum(
        group_torque(group, refs[:peers], ref_beams, keep, weight, *refs[peers + 4 : peers + 8])
        for group in range(groups)
    )
    unit, step = pl.program_id(0), pl.program_id(1)

    @pl.when((unit == 0) & (step == 0))
    def _():
        for new, old in zip(out, before):
            new[...] = old[...]
        if not before:
            for new in out:
                new[...] = jnp.zeros_like(new)

    unit = unit + low
    out[0][unit % out[0].shape[0]] += torque * scales[unit]
    out[1][unit] += jnp.sum(torque, 0, keepdims=True)


def unit_torque(blocks, offsets, ref_beams, keep, weight, scales, tables, low, high, before):
    peers = len(blocks)
    block_times, width = blocks[0].shape[2:]
    chans, pols = ref_beams.shape[2:4]
    sums = ((pols, CYL, NSF), (chans * pols, 1, NSF))
    whole = lambda shape: pl.BlockSpec(
        shape, lambda u, g: (0,) * len(shape), pipeline_mode=pl.Buffered(1)
    )
    unit = lambda offset: (lambda u, g: (0, u + offset, g, 0))
    groups = min(GROUPS, block_times // ROWS)
    times = groups * ROWS
    return pl.pallas_call(
        lambda *refs: beam_kernel(peers, groups, low, *refs),
        grid=(high - low, block_times // times),
        in_specs=[pl.BlockSpec((2, 1, times, width), unit(offset)) for offset in offsets]
        + [
            pl.BlockSpec(
                (2, times, 1, 1, EWB, NSB),
                lambda u, g: (0, g, (u + low) // pols, (u + low) % pols, 0, 0),
            ),
            pl.BlockSpec((1, times, LANES), lambda u, g: ((u + low) // pols, g, 0)),
            whole(weight.shape),
            pl.BlockSpec(memory_space=pltpu.SMEM),
        ]
        + [whole(t.shape) for t in tables]
        + [whole(b.shape) for b in before],
        out_specs=[pl.BlockSpec(s, lambda u, g: (0, 0, 0)) for s in sums],
        out_shape=[jax.ShapeDtypeStruct(s, jnp.float32) for s in sums],
        compiler_params=pltpu.CompilerParams(vmem_limit_bytes=48 << 20),
        name="beams",
    )(*blocks, ref_beams, keep, weight, scales, *tables, *before)


def shards(voltages, beam_refs, beam_weight, delays, band_phase, rfi_flags, grid_rows):
    _, local_times, local_chans, pol_count, width = voltages.shape
    peers = lax.axis_size("feed")
    me = lax.axis_index("feed")
    others = lax.axis_size("chan") * lax.axis_size("tm")
    times_total = local_times * lax.axis_size("tm")
    chans_total = local_chans * lax.axis_size("chan")
    block_times = local_times // peers
    span = width // CYL
    partners = me ^ jnp.arange(peers, dtype=jnp.int32)
    chan_index = (
        lax.axis_index("chan") * local_chans + jnp.arange(local_chans, dtype=jnp.int32)
    ).astype(jnp.float32)
    frequency = 0.4 + 0.4 * (chan_index + 0.5) / chans_total
    basis = band_basis(chan_index, chans_total)
    voltages, delays, band_phase = (
        pltpu.with_memory_space_constraint(a, pltpu.HBM) for a in (voltages, delays, band_phase)
    )

    units = local_chans * pol_count
    middle = units // 2
    ends = [0, middle, units - 2, units - 1, units]
    chunks = list(zip(ends[:-1], ends[1:]))
    blocks = [[None] * peers for _ in chunks]
    offsets = [[0] * peers for _ in chunks]

    made = {}
    for kind, group, part, piece in issue_plan(peers):
        mine = [i for i, (low, _) in enumerate(chunks) if (low >= middle) == part]
        remote = group[0] >= peers // 2
        cuts = [chunks[i][0] - part * middle for i in mine] + [middle]
        if kind == "sky":
            cuts = cuts if remote else [0, middle]
            blocks_made = sky_blocks(
                voltages, delays, band_phase, peers, group, part, cuts, chans_total
            )
            for partner, pieces in zip(group, blocks_made):
                made[partner, part] = pieces
            continue
        partner = group[0]
        block = made[partner, part][piece]
        if partner:
            pairs = [(i, i ^ partner) for i in range(peers)]
            block = lax.ppermute(block, "feed", pairs)
        for at, i in enumerate(mine):
            if at == piece or not remote:
                blocks[i][partner] = block
                offsets[i][partner] = 0 if remote else cuts[at]

    rows = grid_rows.reshape(peers, -1)[partners].reshape(-1)
    north_fwd = north_table(rows)
    east_fwd, east_adj = east_tables()
    tables = (east_fwd, east_adj, north_fwd, north_fwd.T)
    flags = lax.dynamic_slice_in_dim(rfi_flags, me * block_times, block_times, 0)
    keep = (1 - flags).astype(jnp.float32).T
    keep = jnp.broadcast_to(keep[:, :, None], (local_chans, block_times, LANES))
    ref_beams = beam_refs.reshape(2, block_times, local_chans, pol_count, EWB, NSB)
    scales = jnp.repeat(full_turn * frequency, pol_count)
    sums = ()
    for i, (low, high) in enumerate(chunks):
        sums = unit_torque(
            blocks[i], offsets[i], ref_beams, keep, beam_weight, scales, tables, low, high, sums
        )
    delay_part = sums[0] / times_total
    chan_part = jnp.sum(sums[1], axis=(1, 2)).reshape(local_chans, pol_count) / times_total
    band_part = jnp.sum(chan_part[:, :, None] * basis[:, None, :], 0)
    delay_part = delay_part.reshape(pol_count, CYL, peers, span)
    delay_part = jnp.transpose(delay_part, (2, 0, 3, 1)).reshape(peers, -1, LANES)
    delay_part = delay_part[partners]
    band_part = jnp.pad(band_part.reshape(-1), (0, LANES - band_part.size))
    band_part = jnp.broadcast_to(band_part[None, None], (peers, 1, LANES))
    slots = jnp.concatenate([delay_part, band_part], 1)
    slots = jnp.broadcast_to(slots[:, None], (peers, others) + slots.shape[1:])
    slots = slots.reshape((peers * others,) + slots.shape[2:])
    total = jnp.sum(lax.all_to_all(slots, ("feed", "chan", "tm"), 0, 0, tiled=True), 0)
    return (
        total[:-1].reshape(pol_count, width),
        total[-1, : pol_count * BANDS].reshape(pol_count, BANDS),
    )


def issue_plan(peers):
    far = list(range(peers // 2, peers))
    near = list(range(1, peers // 2))
    plan = []
    for part, pieces in enumerate((1, 3)):
        groups = [far[:1], far[1:]] if part == 0 else [far]
        for group in groups:
            plan.append(("sky", group, part, 0))
            plan += [("send", [partner], part, 0) for partner in group]
        plan.append(("sky", near + [0], part, 0))
        plan += [("send", [partner], part, 0) for partner in near + [0]]
        plan += [
            ("send", [partner], part, piece) for piece in range(1, pieces) for partner in far
        ]
    return plan


def solution(mesh):
    in_specs = (
        P(None, "tm", "chan", None, "feed"),
        P(None, "tm", "feed", None, "chan", None, None, None),
        P(),
        P(None, "feed"),
        P(),
        P("tm", "chan"),
        P(),
    )
    out_specs = (P(None, "feed"), P())

    return jax.shard_map(shards, mesh=mesh, in_specs=in_specs, out_specs=out_specs, check_vma=False)
```

```python
import math

import jax
import jax.numpy as jnp
import numpy as np
from jax import lax
from jax.experimental import pallas as pl
from jax.experimental.pallas import tpu as pltpu
from jax.sharding import PartitionSpec as P

CYL = 16
NSF = 256
EWB = 32
NSB = 512
BANDS = 16
ROWS = 8
GROUPS = 4
BATCH = 4
LANES = 128


full_turn = 2.0 * math.pi


def east_tables():
    angle = np.float32(full_turn / EWB) * (
        np.arange(EWB)[:, None] * np.arange(CYL)[None, :] % EWB
    ).astype(np.float32)
    real = np.cos(angle) / np.float32(math.sqrt(EWB))
    imag = -np.sin(angle) / np.float32(math.sqrt(EWB))
    parts = np.array([[real, -imag], [imag, real]], np.float32)
    same = np.eye(ROWS, dtype=np.float32)
    forward = np.einsum("abec,rs->arebcs", parts, same)
    forward = forward.reshape(2 * ROWS * EWB, 2 * CYL * ROWS)
    return jnp.asarray(forward, jnp.bfloat16), jnp.asarray(forward.T, jnp.bfloat16)


def north_parts():
    angle = np.float32(full_turn / NSB) * (
        np.arange(NSB)[:, None] * np.arange(NSF)[None, :] % NSB
    ).astype(np.float32)
    parts = np.stack([np.cos(angle), -np.sin(angle)]) / np.float32(math.sqrt(NSB))
    return jnp.asarray(parts, jnp.bfloat16)


def north_kernel(rows, parts, forward, adjoint):
    row = lax.broadcasted_iota(jnp.int32, (NSF, NSF), 0)
    chosen = jnp.where(row == rows[...], 1.0, 0.0)
    columns = chosen.astype(jnp.bfloat16)
    lines = chosen.T.astype(jnp.bfloat16)
    for part in range(2):
        table = parts[part]
        wide = jnp.dot(table, columns, preferred_element_type=jnp.float32)
        tall = lax.dot_general(
            lines, table, (((1,), (1,)), ((), ())), preferred_element_type=jnp.float32
        )
        same, swap = (lambda i: slice(i * NSB, (i + 1) * NSB)), (lambda i: slice(i * NSF, (i + 1) * NSF))
        for other in range(2):
            sign = -1.0 if part and other else 1.0
            m, n = same(part ^ other), swap(other)
            adjoint[m, n] = (sign * wide).astype(jnp.bfloat16)
            forward[n, m] = (sign * tall).astype(jnp.bfloat16)


def north_tables(rows):
    return pl.pallas_call(
        north_kernel,
        out_shape=[
            pltpu.VMEM((2 * NSF, 2 * NSB), jnp.bfloat16),
            pltpu.VMEM((2 * NSB, 2 * NSF), jnp.bfloat16),
        ],
        name="north",
    )(rows.reshape(1, NSF), north_parts())


def band_basis(chan_index, chans_total):
    term_index = jnp.arange(BANDS).astype(jnp.float32)
    return math.sqrt(2.0 / chans_total) * jnp.cos(
        math.pi * (chan_index[:, None] + 0.5) * term_index[None, :] / chans_total
    )


def sky_kernel(partners, cuts, span, chan_start, chans_total, volts, delay_ref, band_ref, *refs):
    outs, (delays, band_phase, held, order, small, arrived) = refs[:-6], refs[-6:]
    _, _, times, chans, pols, width = held.shape
    me = lax.axis_index("feed")
    first_chan = lax.axis_index("chan") * volts.shape[2] + chan_start
    tables = [
        pltpu.make_async_copy(delay_ref, delays, small.at[0]),
        pltpu.make_async_copy(band_ref, band_phase, small.at[1]),
    ]
    for copy in tables:
        copy.start()
    copies = [
        pltpu.make_async_copy(
            volts.at[:, pl.ds((me ^ partner) * times, times), pl.ds(chan_start, chans)],
            held.at[index],
            arrived.at[index],
        )
        for index, partner in enumerate(partners)
    ]
    for copy in copies:
        copy.start()
    row = lax.broadcasted_iota(jnp.int32, (width, width), 0)
    column = lax.broadcasted_iota(jnp.int32, (width, width), 1)
    target = (row % CYL) * span + row // CYL
    order[...] = jnp.where(target == column, 1.0, 0.0).astype(jnp.bfloat16)
    term = lax.broadcasted_iota(jnp.int32, (1, BANDS), 1).astype(jnp.float32)
    for copy in tables:
        copy.wait()
    phases = []
    for chan in range(chans):
        place = (first_chan + chan).astype(jnp.float32)
        frequency = 0.4 + 0.4 * (place + 0.5) / chans_total
        basis = math.sqrt(2.0 / chans_total) * jnp.cos(
            math.pi * (place + 0.5) * term / chans_total
        )
        offset = jnp.sum(band_phase[...] * basis, 1, keepdims=True)
        phases.append(full_turn * frequency * delays[...] + offset)
    phases = jnp.concatenate(phases, 0)
    cosine, sine = jnp.cos(phases), -jnp.sin(phases)
    for index, partner in enumerate(partners):
        copies[index].wait()
        for chan in range(chans):
            block = held[index, :, :, chan].astype(jnp.float32)
            for pol in range(pols):
                unit = chan * pols + pol
                real, imag = block[0, :, pol], block[1, :, pol]
                gr, gi = cosine[unit : unit + 1], sine[unit : unit + 1]
                both = jnp.concatenate([gr * real - gi * imag, gr * imag + gi * real], 0)
                both = jnp.dot(
                    both.astype(jnp.bfloat16), order[...], preferred_element_type=jnp.float32
                )
                shift = partner * span % LANES
                if shift:
                    both = jnp.concatenate(
                        [
                            pltpu.roll(both[:, at : at + LANES], shift, 1)
                            for at in range(0, width, LANES)
                        ],
                        1,
                    )
                both = both.astype(jnp.bfloat16)
                piece = sum(unit >= cut for cut in cuts[1:-1])
                out = outs[index * (len(cuts) - 1) + piece]
                out[0, unit - cuts[piece]] = both[:times]
                out[1, unit - cuts[piece]] = both[times:]


def sky_blocks(voltages, delays, band_phase, peers, partners, part, cuts, chans_total):
    _, times, chans, pols, width = voltages.shape
    block = times // peers
    half = chans // 2
    outs = [
        jax.ShapeDtypeStruct((2, high - low, block, width), jnp.bfloat16)
        for _ in partners
        for low, high in zip(cuts[:-1], cuts[1:])
    ]
    result = pl.pallas_call(
        lambda *refs: sky_kernel(partners, cuts, width // CYL, part * half, chans_total, *refs),
        in_specs=[pl.BlockSpec(memory_space=pl.ANY)] * 3,
        out_specs=[pl.BlockSpec(memory_space=pltpu.VMEM)] * len(outs),
        scratch_shapes=[
            pltpu.VMEM(delays.shape, delays.dtype),
            pltpu.VMEM(band_phase.shape, band_phase.dtype),
            pltpu.VMEM((len(partners), 2, block, half, pols, width), jnp.bfloat16),
            pltpu.VMEM((width, width), jnp.bfloat16),
            pltpu.SemaphoreType.DMA((2,)),
            pltpu.SemaphoreType.DMA((len(partners),)),
        ],
        out_shape=outs,
        compiler_params=pltpu.CompilerParams(vmem_limit_bytes=48 << 20),
        name="sky",
    )(voltages, delays, band_phase)
    pieces = len(cuts) - 1
    return [result[i * pieces : (i + 1) * pieces] for i in range(len(partners))]


def group_sky(group, blocks):
    peers, width = len(blocks), blocks[0].shape[-1]
    span = width // CYL
    per_tile = LANES // span
    times = slice(group * ROWS, (group + 1) * ROWS)
    lane = lax.broadcasted_iota(jnp.int32, (ROWS, LANES), 1) // span
    pieces = []
    for part in range(2):
        loaded = [blocks[k][part, 0, times].astype(jnp.float32) for k in range(peers)]
        for c in range(CYL):
            tile, turn = divmod(c, per_tile)
            at = tile * LANES
            for half in range(NSF // LANES):
                value = None
                for slot in range(per_tile):
                    piece = loaded[half * per_tile + slot][:, at : at + LANES]
                    spot = (turn + slot) % per_tile
                    value = piece if value is None else jnp.where(lane == spot, piece, value)
                if turn:
                    value = pltpu.roll(value, LANES - turn * span, 1)
                pieces.append(value)
    return jnp.concatenate(
        [jnp.concatenate(pieces[i : i + 2], 1) for i in range(0, len(pieces), 2)], 0
    )


def batch_torque(groups, blocks, ref_beams, keep, weight, east_fwd, east_adj, north_fwd, north_adj):
    half = ROWS * EWB
    span = slice(groups[0] * ROWS, (groups[-1] + 1) * ROWS)
    skies, easts = [], []
    for group in groups:
        sky = group_sky(group, blocks).astype(jnp.bfloat16)
        east = jnp.dot(east_fwd[...], sky, preferred_element_type=jnp.float32)
        east = east.astype(jnp.bfloat16)
        skies.append(sky)
        easts.append(jnp.concatenate([east[:half], east[half:]], 1))
    beams = jnp.dot(
        jnp.concatenate(easts, 0), north_fwd[...], preferred_element_type=jnp.float32
    ).reshape(len(groups) * ROWS, EWB, 2 * NSB)
    residual = jnp.concatenate(
        [
            (
                (beams[:, :, part * NSB : (part + 1) * NSB] - ref_beams[part, span, 0, 0].astype(jnp.float32))
                * weight[...][None]
            ).astype(jnp.bfloat16)
            for part in range(2)
        ],
        2,
    ).reshape(len(groups) * half, 2 * NSB)
    backs = jnp.dot(residual, north_adj[...], preferred_element_type=jnp.float32)
    backs = backs.astype(jnp.bfloat16)
    rows = CYL * ROWS
    total = 0.0
    for at, group in enumerate(groups):
        back = backs[at * half : (at + 1) * half]
        back = jnp.concatenate([back[:, :NSF], back[:, NSF:]], 0)
        field = jnp.dot(east_adj[...], back, preferred_element_type=jnp.float32)
        sky = skies[at].astype(jnp.float32)
        torque = field[:rows] * sky[rows:] - field[rows:] * sky[:rows]
        kept = keep[0, group * ROWS : (group + 1) * ROWS][None, :, :1]
        total += jnp.sum(torque.reshape(CYL, ROWS, NSF) * kept, 1)
    return total


def beam_kernel(peers, groups, low, *refs):
    ref_beams, keep, weight, scales = refs[peers : peers + 4]
    before, out = refs[peers + 8 : -2], refs[-2:]
    torque = sum(
        batch_torque(
            range(first, min(first + BATCH, groups)),
            refs[:peers],
            ref_beams,
            keep,
            weight,
            *refs[peers + 4 : peers + 8],
        )
        for first in range(0, groups, BATCH)
    )
    unit, step = pl.program_id(0), pl.program_id(1)

    @pl.when((unit == 0) & (step == 0))
    def _():
        for new, old in zip(out, before):
            new[...] = old[...]
        if not before:
            for new in out:
                new[...] = jnp.zeros_like(new)

    unit = unit + low
    out[0][unit % out[0].shape[0]] += torque * scales[unit]
    out[1][unit] += jnp.sum(torque, 0, keepdims=True)


def unit_torque(blocks, offsets, ref_beams, keep, weight, scales, tables, low, high, before):
    peers = len(blocks)
    block_times, width = blocks[0].shape[2:]
    chans, pols = ref_beams.shape[2:4]
    sums = ((pols, CYL, NSF), (chans * pols, 1, NSF))
    whole = lambda shape: pl.BlockSpec(
        shape, lambda u, g: (0,) * len(shape), pipeline_mode=pl.Buffered(1)
    )
    unit = lambda offset: (lambda u, g: (0, u + offset, g, 0))
    groups = min(GROUPS, block_times // ROWS)
    times = groups * ROWS
    return pl.pallas_call(
        lambda *refs: beam_kernel(peers, groups, low, *refs),
        grid=(high - low, block_times // times),
        in_specs=[pl.BlockSpec((2, 1, times, width), unit(offset)) for offset in offsets]
        + [
            pl.BlockSpec(
                (2, times, 1, 1, EWB, NSB),
                lambda u, g: (0, g, (u + low) // pols, (u + low) % pols, 0, 0),
            ),
            pl.BlockSpec((1, times, LANES), lambda u, g: ((u + low) // pols, g, 0)),
            whole(weight.shape),
            pl.BlockSpec(memory_space=pltpu.SMEM),
        ]
        + [whole(t.shape) for t in tables]
        + [whole(b.shape) for b in before],
        out_specs=[pl.BlockSpec(s, lambda u, g: (0, 0, 0)) for s in sums],
        out_shape=[jax.ShapeDtypeStruct(s, jnp.float32) for s in sums],
        compiler_params=pltpu.CompilerParams(vmem_limit_bytes=48 << 20),
        name="beams",
    )(*blocks, ref_beams, keep, weight, scales, *tables, *before)


def shards(voltages, beam_refs, beam_weight, delays, band_phase, rfi_flags, grid_rows):
    _, local_times, local_chans, pol_count, width = voltages.shape
    peers = lax.axis_size("feed")
    me = lax.axis_index("feed")
    others = lax.axis_size("chan") * lax.axis_size("tm")
    times_total = local_times * lax.axis_size("tm")
    chans_total = local_chans * lax.axis_size("chan")
    block_times = local_times // peers
    span = width // CYL
    partners = me ^ jnp.arange(peers, dtype=jnp.int32)
    chan_index = (
        lax.axis_index("chan") * local_chans + jnp.arange(local_chans, dtype=jnp.int32)
    ).astype(jnp.float32)
    frequency = 0.4 + 0.4 * (chan_index + 0.5) / chans_total
    basis = band_basis(chan_index, chans_total)
    voltages, delays, band_phase = (
        pltpu.with_memory_space_constraint(a, pltpu.HBM) for a in (voltages, delays, band_phase)
    )

    units = local_chans * pol_count
    middle = units // 2
    ends = [0, middle, units - 2, units]
    chunks = list(zip(ends[:-1], ends[1:]))
    blocks = [[None] * peers for _ in chunks]
    offsets = [[0] * peers for _ in chunks]

    made = {}
    for kind, group, part, piece in issue_plan(peers):
        mine = [i for i, (low, _) in enumerate(chunks) if (low >= middle) == part]
        remote = group[0] >= peers // 2
        cuts = [chunks[i][0] - part * middle for i in mine] + [middle]
        if kind == "sky":
            cuts = cuts if remote else [0, middle]
            blocks_made = sky_blocks(
                voltages, delays, band_phase, peers, group, part, cuts, chans_total
            )
            for partner, pieces in zip(group, blocks_made):
                made[partner, part] = pieces
            continue
        partner = group[0]
        block = made[partner, part][piece]
        if partner:
            pairs = [(i, i ^ partner) for i in range(peers)]
            block = lax.ppermute(block, "feed", pairs)
        for at, i in enumerate(mine):
            if at == piece or not remote:
                blocks[i][partner] = block
                offsets[i][partner] = 0 if remote else cuts[at]

    rows = grid_rows.reshape(peers, -1)[partners].reshape(-1)
    north_fwd, north_adj = north_tables(rows)
    east_fwd, east_adj = east_tables()
    tables = (east_fwd, east_adj, north_fwd, north_adj)
    flags = lax.dynamic_slice_in_dim(rfi_flags, me * block_times, block_times, 0)
    keep = (1 - flags).astype(jnp.float32).T
    keep = jnp.broadcast_to(keep[:, :, None], (local_chans, block_times, LANES))
    ref_beams = beam_refs.reshape(2, block_times, local_chans, pol_count, EWB, NSB)
    scales = jnp.repeat(full_turn * frequency, pol_count)
    sums = ()
    for i, (low, high) in enumerate(chunks):
        sums = unit_torque(
            blocks[i], offsets[i], ref_beams, keep, beam_weight, scales, tables, low, high, sums
        )
    delay_part = sums[0] / times_total
    chan_part = jnp.sum(sums[1], axis=(1, 2)).reshape(local_chans, pol_count) / times_total
    band_part = jnp.sum(chan_part[:, :, None] * basis[:, None, :], 0)
    delay_part = delay_part.reshape(pol_count, CYL, peers, span)
    delay_part = jnp.transpose(delay_part, (2, 0, 3, 1)).reshape(peers, -1, LANES)
    delay_part = delay_part[partners]
    band_part = jnp.pad(band_part.reshape(-1), (0, LANES - band_part.size))
    band_part = jnp.broadcast_to(band_part[None, None], (peers, 1, LANES))
    slots = jnp.concatenate([delay_part, band_part], 1)
    slots = jnp.broadcast_to(slots[:, None], (peers, others) + slots.shape[1:])
    slots = slots.reshape((peers * others,) + slots.shape[2:])
    total = jnp.sum(lax.all_to_all(slots, ("feed", "chan", "tm"), 0, 0, tiled=True), 0)
    return (
        total[:-1].reshape(pol_count, width),
        total[-1, : pol_count * BANDS].reshape(pol_count, BANDS),
    )


def halves(peers):
    return list(range(peers - 1, peers // 2, -2)) + list(range(peers - 2, peers // 2 - 1, -2)), list(range(1, peers // 2))


def issue_plan(peers):
    far, near = halves(peers)
    send = lambda group, part, piece=0: [("send", [partner], part, piece) for partner in group]
    return (
        [("sky", far[:1], 0, 0)]
        + send(far[:1], 0)
        + [("sky", far[1:], 0, 0)]
        + send(far[1:], 0)
        + [("sky", near + [0], 0, 0)]
        + send(near + [0], 0)
        + [("sky", near + [0], 1, 0)]
        + send(near + [0], 1)
        + [("sky", far, 1, 0)]
        + send(far, 1)
        + send(far, 1, 1)
    )


def solution(mesh):
    in_specs = (
        P(None, "tm", "chan", None, "feed"),
        P(None, "tm", "feed", None, "chan", None, None, None),
        P(),
        P(None, "feed"),
        P(),
        P("tm", "chan"),
        P(),
    )
    out_specs = (P(None, "feed"), P())

    return jax.shard_map(shards, mesh=mesh, in_specs=in_specs, out_specs=out_specs, check_vma=False)
```

```python
import math

import jax
import jax.numpy as jnp
import numpy as np
from jax import lax
from jax.experimental import pallas as pl
from jax.experimental.pallas import tpu as pltpu
from jax.sharding import PartitionSpec as P

CYL = 16
NSF = 256
EWB = 32
NSB = 512
BANDS = 16
ROWS = 8
GROUPS = 4
BATCH = 4
LANES = 128


full_turn = 2.0 * math.pi


def east_tables():
    angle = np.float32(full_turn / EWB) * (
        np.arange(EWB)[:, None] * np.arange(CYL)[None, :] % EWB
    ).astype(np.float32)
    real = np.cos(angle) / np.float32(math.sqrt(EWB))
    imag = -np.sin(angle) / np.float32(math.sqrt(EWB))
    parts = np.array([[real, -imag], [imag, real]], np.float32)
    same = np.eye(ROWS, dtype=np.float32)
    forward = np.einsum("abec,rs->arebcs", parts, same)
    forward = forward.reshape(2 * ROWS * EWB, 2 * CYL * ROWS)
    return jnp.asarray(forward, jnp.bfloat16), jnp.asarray(forward.T, jnp.bfloat16)


def north_parts():
    angle = np.float32(full_turn / NSB) * (
        np.arange(NSB)[:, None] * np.arange(NSF)[None, :] % NSB
    ).astype(np.float32)
    parts = np.stack([np.cos(angle), -np.sin(angle)]) / np.float32(math.sqrt(NSB))
    return jnp.asarray(parts, jnp.bfloat16)


def north_kernel(rows, parts, forward, adjoint):
    row = lax.broadcasted_iota(jnp.int32, (NSF, NSF), 0)
    chosen = jnp.where(row == rows[...], 1.0, 0.0)
    columns = chosen.astype(jnp.bfloat16)
    lines = chosen.T.astype(jnp.bfloat16)
    for part in range(2):
        table = parts[part]
        wide = jnp.dot(table, columns, preferred_element_type=jnp.float32)
        tall = lax.dot_general(
            lines, table, (((1,), (1,)), ((), ())), preferred_element_type=jnp.float32
        )
        same, swap = (lambda i: slice(i * NSB, (i + 1) * NSB)), (lambda i: slice(i * NSF, (i + 1) * NSF))
        for other in range(2):
            sign = -1.0 if part and other else 1.0
            m, n = same(part ^ other), swap(other)
            adjoint[m, n] = (sign * wide).astype(jnp.bfloat16)
            forward[n, m] = (sign * tall).astype(jnp.bfloat16)


def north_tables(rows):
    return pl.pallas_call(
        north_kernel,
        out_shape=[
            pltpu.VMEM((2 * NSF, 2 * NSB), jnp.bfloat16),
            pltpu.VMEM((2 * NSB, 2 * NSF), jnp.bfloat16),
        ],
        name="north",
    )(rows.reshape(1, NSF), north_parts())


def band_basis(chan_index, chans_total):
    term_index = jnp.arange(BANDS).astype(jnp.float32)
    return math.sqrt(2.0 / chans_total) * jnp.cos(
        math.pi * (chan_index[:, None] + 0.5) * term_index[None, :] / chans_total
    )


def sky_kernel(partners, cuts, span, chan_start, chans_total, volts, delay_ref, band_ref, *refs):
    outs, (delays, band_phase, held, order, small, arrived) = refs[:-6], refs[-6:]
    _, _, times, chans, pols, width = held.shape
    me = lax.axis_index("feed")
    first_chan = lax.axis_index("chan") * volts.shape[2] + chan_start
    tables = [
        pltpu.make_async_copy(delay_ref, delays, small.at[0]),
        pltpu.make_async_copy(band_ref, band_phase, small.at[1]),
    ]
    for copy in tables:
        copy.start()
    copies = [
        pltpu.make_async_copy(
            volts.at[:, pl.ds((me ^ partner) * times, times), pl.ds(chan_start, chans)],
            held.at[index],
            arrived.at[index],
        )
        for index, partner in enumerate(partners)
    ]
    for copy in copies:
        copy.start()
    row = lax.broadcasted_iota(jnp.int32, (width, width), 0)
    column = lax.broadcasted_iota(jnp.int32, (width, width), 1)
    target = (row % CYL) * span + row // CYL
    order[...] = jnp.where(target == column, 1.0, 0.0).astype(jnp.bfloat16)
    term = lax.broadcasted_iota(jnp.int32, (1, BANDS), 1).astype(jnp.float32)
    for copy in tables:
        copy.wait()
    phases = []
    for chan in range(chans):
        place = (first_chan + chan).astype(jnp.float32)
        frequency = 0.4 + 0.4 * (place + 0.5) / chans_total
        basis = math.sqrt(2.0 / chans_total) * jnp.cos(
            math.pi * (place + 0.5) * term / chans_total
        )
        offset = jnp.sum(band_phase[...] * basis, 1, keepdims=True)
        phases.append(full_turn * frequency * delays[...] + offset)
    phases = jnp.concatenate(phases, 0)
    cosine, sine = jnp.cos(phases), -jnp.sin(phases)
    for index, partner in enumerate(partners):
        copies[index].wait()
        for chan in range(chans):
            block = held[index, :, :, chan].astype(jnp.float32)
            for pol in range(pols):
                unit = chan * pols + pol
                real, imag = block[0, :, pol], block[1, :, pol]
                gr, gi = cosine[unit : unit + 1], sine[unit : unit + 1]
                both = jnp.concatenate([gr * real - gi * imag, gr * imag + gi * real], 0)
                both = jnp.dot(
                    both.astype(jnp.bfloat16), order[...], preferred_element_type=jnp.float32
                )
                shift = partner * span % LANES
                if shift:
                    both = jnp.concatenate(
                        [
                            pltpu.roll(both[:, at : at + LANES], shift, 1)
                            for at in range(0, width, LANES)
                        ],
                        1,
                    )
                both = both.astype(jnp.bfloat16)
                piece = sum(unit >= cut for cut in cuts[1:-1])
                out = outs[index * (len(cuts) - 1) + piece]
                out[0, unit - cuts[piece]] = both[:times]
                out[1, unit - cuts[piece]] = both[times:]


def sky_blocks(voltages, delays, band_phase, peers, partners, part, cuts, chans_total):
    _, times, chans, pols, width = voltages.shape
    block = times // peers
    half = chans // 2
    outs = [
        jax.ShapeDtypeStruct((2, high - low, block, width), jnp.bfloat16)
        for _ in partners
        for low, high in zip(cuts[:-1], cuts[1:])
    ]
    result = pl.pallas_call(
        lambda *refs: sky_kernel(partners, cuts, width // CYL, part * half, chans_total, *refs),
        in_specs=[pl.BlockSpec(memory_space=pl.ANY)] * 3,
        out_specs=[pl.BlockSpec(memory_space=pltpu.VMEM)] * len(outs),
        scratch_shapes=[
            pltpu.VMEM(delays.shape, delays.dtype),
            pltpu.VMEM(band_phase.shape, band_phase.dtype),
            pltpu.VMEM((len(partners), 2, block, half, pols, width), jnp.bfloat16),
            pltpu.VMEM((width, width), jnp.bfloat16),
            pltpu.SemaphoreType.DMA((2,)),
            pltpu.SemaphoreType.DMA((len(partners),)),
        ],
        out_shape=outs,
        compiler_params=pltpu.CompilerParams(vmem_limit_bytes=48 << 20),
        name="sky",
    )(voltages, delays, band_phase)
    pieces = len(cuts) - 1
    return [result[i * pieces : (i + 1) * pieces] for i in range(len(partners))]


def group_sky(group, blocks):
    peers, width = len(blocks), blocks[0].shape[-1]
    span = width // CYL
    per_tile = LANES // span
    times = slice(group * ROWS, (group + 1) * ROWS)
    lane = lax.broadcasted_iota(jnp.int32, (ROWS, LANES), 1) // span
    pieces = []
    for part in range(2):
        loaded = [blocks[k][part, 0, times].astype(jnp.float32) for k in range(peers)]
        for c in range(CYL):
            tile, turn = divmod(c, per_tile)
            at = tile * LANES
            for half in range(NSF // LANES):
                value = None
                for slot in range(per_tile):
                    piece = loaded[half * per_tile + slot][:, at : at + LANES]
                    spot = (turn + slot) % per_tile
                    value = piece if value is None else jnp.where(lane == spot, piece, value)
                if turn:
                    value = pltpu.roll(value, LANES - turn * span, 1)
                pieces.append(value)
    return jnp.concatenate(
        [jnp.concatenate(pieces[i : i + 2], 1) for i in range(0, len(pieces), 2)], 0
    )


def batch_torque(groups, blocks, ref_beams, keep, weight, east_fwd, east_adj, north_fwd, north_adj):
    half = ROWS * EWB
    span = slice(groups[0] * ROWS, (groups[-1] + 1) * ROWS)
    skies, easts = [], []
    for group in groups:
        sky = group_sky(group, blocks).astype(jnp.bfloat16)
        east = jnp.dot(east_fwd[...], sky, preferred_element_type=jnp.float32)
        east = east.astype(jnp.bfloat16)
        skies.append(sky)
        easts.append(jnp.concatenate([east[:half], east[half:]], 1))
    beams = jnp.dot(
        jnp.concatenate(easts, 0), north_fwd[...], preferred_element_type=jnp.float32
    ).reshape(len(groups) * ROWS, EWB, 2 * NSB)
    residual = jnp.concatenate(
        [
            (
                (beams[:, :, part * NSB : (part + 1) * NSB] - ref_beams[part, span, 0, 0].astype(jnp.float32))
                * weight[...][None]
            ).astype(jnp.bfloat16)
            for part in range(2)
        ],
        2,
    ).reshape(len(groups) * half, 2 * NSB)
    backs = jnp.dot(residual, north_adj[...], preferred_element_type=jnp.float32)
    backs = backs.astype(jnp.bfloat16)
    rows = CYL * ROWS
    total = 0.0
    for at, group in enumerate(groups):
        back = backs[at * half : (at + 1) * half]
        back = jnp.concatenate([back[:, :NSF], back[:, NSF:]], 0)
        field = jnp.dot(east_adj[...], back, preferred_element_type=jnp.float32)
        sky = skies[at].astype(jnp.float32)
        torque = field[:rows] * sky[rows:] - field[rows:] * sky[:rows]
        kept = keep[0, group * ROWS : (group + 1) * ROWS][None, :, :1]
        total += jnp.sum(torque.reshape(CYL, ROWS, NSF) * kept, 1)
    return total


def pack(sums, shares, slots, peers, others, span):
    per_tile = LANES // span
    rows = CYL // per_tile
    me = lax.axis_index("feed")
    lane = lax.broadcasted_iota(jnp.int32, (rows, LANES), 1) // span
    band = sum(
        shares[unit : unit + 1] * jnp.sum(sums[1][unit], keepdims=True)
        for unit in range(sums[1].shape[0])
    )
    for partner in range(peers):
        half, slot = divmod(partner, per_tile)
        block = []
        for pol in range(sums[0].shape[0]):
            tile = sums[0][pol][:, half * LANES : (half + 1) * LANES]
            value = None
            for spot in range(per_tile):
                shift = (spot - slot) * span % LANES
                piece = pltpu.roll(tile, shift, 1) if shift else tile
                piece = piece[spot * rows : (spot + 1) * rows]
                value = piece if value is None else jnp.where(lane == spot, piece, value)
            block.append(value)
        lines = [value[row : row + 1] for value in block for row in range(rows)] + [band]
        for other in range(others):
            for at, line in enumerate(lines):
                slots[(me ^ partner) * others + other, :, at * LANES : (at + 1) * LANES] = line


def unpack_kernel(slots, delay_grad, band_grad):
    pols, width = delay_grad.shape
    span = width // CYL
    rows = CYL * span // LANES
    total = slots[0]
    for other in range(1, slots.shape[0]):
        total += slots[other]
    parts, rest = [], total
    for _ in range(3):
        parts.append(rest.astype(jnp.bfloat16).astype(jnp.float32))
        rest = rest - parts[-1]
    lane = lax.broadcasted_iota(jnp.int32, (LANES, width), 0)
    feed = lax.broadcasted_iota(jnp.int32, (LANES, width), 1)
    where = (lane % span) * CYL + (lane // span) * rows
    moved = 0.0
    for row in range(rows):
        chosen = jnp.where(where + row == feed, 1.0, 0.0).astype(jnp.bfloat16)
        lines = jnp.concatenate(
            [
                part[:, (pol * rows + row) * LANES : (pol * rows + row + 1) * LANES]
                for pol in range(pols)
                for part in parts
            ],
            0,
        )
        moved += jnp.dot(lines.astype(jnp.bfloat16), chosen, preferred_element_type=jnp.float32)
    for pol in range(pols):
        first, second, third = (moved[pol * 3 + i : pol * 3 + i + 1] for i in range(3))
        delay_grad[pol : pol + 1] = first + (second + third)
        band = total[:, pols * rows * LANES :]
        shift = -pol * BANDS % LANES
        band = pltpu.roll(band, shift, 1) if shift else band
        band_grad[pol : pol + 1] = band[:, :BANDS]


def beam_kernel(peers, groups, low, pack_for, *refs):
    ref_beams, keep, weight, scales, shares = refs[peers : peers + 5]
    outs = 3 if pack_for else 2
    before, out = refs[peers + 9 : -outs], refs[-outs:]
    torque = sum(
        batch_torque(
            range(first, min(first + BATCH, groups)),
            refs[:peers],
            ref_beams,
            keep,
            weight,
            *refs[peers + 5 : peers + 9],
        )
        for first in range(0, groups, BATCH)
    )
    unit, step = pl.program_id(0), pl.program_id(1)

    @pl.when((unit == 0) & (step == 0))
    def _():
        for new, old in zip(out, before):
            new[...] = old[...]
        if not before:
            for new in out[:2]:
                new[...] = jnp.zeros_like(new)

    unit = unit + low
    out[0][unit % out[0].shape[0]] += torque * scales[unit]
    out[1][unit] += jnp.sum(torque, 0, keepdims=True)
    if pack_for:

        @pl.when((unit - low == pl.num_programs(0) - 1) & (step == pl.num_programs(1) - 1))
        def _():
            pack(out, shares, out[2], peers, pack_for, refs[0].shape[-1] // CYL)


def unit_torque(blocks, offsets, ref_beams, keep, weight, scales, shares, tables, low, high, before, pack_for):
    peers = len(blocks)
    block_times, width = blocks[0].shape[2:]
    chans, pols = ref_beams.shape[2:4]
    sums = ((pols, CYL, NSF), (chans * pols, 1, NSF))
    if pack_for:
        sums += ((peers * pack_for, 1, pols * width + LANES),)
    whole = lambda shape: pl.BlockSpec(
        shape, lambda u, g: (0,) * len(shape), pipeline_mode=pl.Buffered(1)
    )
    unit = lambda offset: (lambda u, g: (0, u + offset, g, 0))
    groups = min(GROUPS, block_times // ROWS)
    times = groups * ROWS
    return pl.pallas_call(
        lambda *refs: beam_kernel(peers, groups, low, pack_for, *refs),
        grid=(high - low, block_times // times),
        in_specs=[pl.BlockSpec((2, 1, times, width), unit(offset)) for offset in offsets]
        + [
            pl.BlockSpec(
                (2, times, 1, 1, EWB, NSB),
                lambda u, g: (0, g, (u + low) // pols, (u + low) % pols, 0, 0),
            ),
            pl.BlockSpec((1, times, LANES), lambda u, g: ((u + low) // pols, g, 0)),
            whole(weight.shape),
            pl.BlockSpec(memory_space=pltpu.SMEM),
            whole(shares.shape),
        ]
        + [whole(t.shape) for t in tables]
        + [whole(b.shape) for b in before],
        out_specs=[pl.BlockSpec(s, lambda u, g: (0, 0, 0)) for s in sums],
        out_shape=[jax.ShapeDtypeStruct(s, jnp.float32) for s in sums],
        compiler_params=pltpu.CompilerParams(vmem_limit_bytes=48 << 20),
        name="beams",
    )(*blocks, ref_beams, keep, weight, scales, shares, *tables, *before)


def shards(voltages, beam_refs, beam_weight, delays, band_phase, rfi_flags, grid_rows):
    _, local_times, local_chans, pol_count, width = voltages.shape
    peers = lax.axis_size("feed")
    me = lax.axis_index("feed")
    others = lax.axis_size("chan") * lax.axis_size("tm")
    times_total = local_times * lax.axis_size("tm")
    chans_total = local_chans * lax.axis_size("chan")
    block_times = local_times // peers
    partners = me ^ jnp.arange(peers, dtype=jnp.int32)
    chan_index = (
        lax.axis_index("chan") * local_chans + jnp.arange(local_chans, dtype=jnp.int32)
    ).astype(jnp.float32)
    frequency = 0.4 + 0.4 * (chan_index + 0.5) / chans_total
    basis = band_basis(chan_index, chans_total)
    voltages, delays, band_phase = (
        pltpu.with_memory_space_constraint(a, pltpu.HBM) for a in (voltages, delays, band_phase)
    )

    units = local_chans * pol_count
    middle = units // 2
    ends = [0, middle, units - 2, units - 1, units]
    chunks = list(zip(ends[:-1], ends[1:]))
    blocks = [[None] * peers for _ in chunks]
    offsets = [[0] * peers for _ in chunks]

    made = {}
    for kind, group, part, piece in issue_plan(peers):
        mine = [i for i, (low, _) in enumerate(chunks) if (low >= middle) == part]
        remote = group[0] >= peers // 2
        cuts = [chunks[i][0] - part * middle for i in mine] + [middle]
        if kind == "sky":
            cuts = cuts if remote else [0, middle]
            blocks_made = sky_blocks(
                voltages, delays, band_phase, peers, group, part, cuts, chans_total
            )
            for partner, pieces in zip(group, blocks_made):
                made[partner, part] = pieces
            continue
        partner = group[0]
        block = made[partner, part][piece]
        if partner:
            pairs = [(i, i ^ partner) for i in range(peers)]
            block = lax.ppermute(block, "feed", pairs)
        for at, i in enumerate(mine):
            if at == piece or not remote:
                blocks[i][partner] = block
                offsets[i][partner] = 0 if remote else cuts[at]

    rows = grid_rows.reshape(peers, -1)[partners].reshape(-1)
    north_fwd, north_adj = north_tables(rows)
    east_fwd, east_adj = east_tables()
    tables = (east_fwd, east_adj, north_fwd, north_adj)
    flags = lax.dynamic_slice_in_dim(rfi_flags, me * block_times, block_times, 0)
    keep = (1 - flags).astype(jnp.float32).T
    keep = jnp.broadcast_to(keep[:, :, None], (local_chans, block_times, LANES))
    ref_beams = beam_refs.reshape(2, block_times, local_chans, pol_count, EWB, NSB)
    scales = jnp.repeat(full_turn * frequency, pol_count) / times_total
    shares = basis[:, None, None, :] * jnp.eye(pol_count)[None, :, :, None] / times_total
    shares = shares.reshape(units, pol_count * BANDS)
    shares = jnp.pad(shares, ((0, 0), (0, LANES - shares.shape[1])))
    sums = ()
    for i, (low, high) in enumerate(chunks):
        pack_for = others if i == len(chunks) - 1 else 0
        sums = unit_torque(
            blocks[i],
            offsets[i],
            ref_beams,
            keep,
            beam_weight,
            scales,
            shares,
            tables,
            low,
            high,
            sums,
            pack_for,
        )
    slots = lax.all_to_all(sums[2], ("feed", "chan", "tm"), 0, 0, tiled=True)
    return pl.pallas_call(
        unpack_kernel,
        out_shape=(
            jax.ShapeDtypeStruct((pol_count, width), jnp.float32),
            jax.ShapeDtypeStruct((pol_count, BANDS), jnp.float32),
        ),
        name="unpack",
    )(slots)


def halves(peers):
    return list(range(peers - 1, peers // 2, -2)) + list(range(peers - 2, peers // 2 - 1, -2)), list(range(1, peers // 2))


def issue_plan(peers):
    far, near = halves(peers)
    send = lambda group, part, piece=0: [("send", [partner], part, piece) for partner in group]
    return (
        [("sky", far[:1], 0, 0)]
        + send(far[:1], 0)
        + [("sky", far[1:], 0, 0)]
        + send(far[1:], 0)
        + [("sky", near + [0], 0, 0)]
        + send(near + [0], 0)
        + [("sky", near + [0], 1, 0)]
        + send(near + [0], 1)
        + [("sky", far, 1, 0)]
        + send(far, 1)
        + send(far, 1, 1)
        + send(far, 1, 2)
    )


def solution(mesh):
    in_specs = (
        P(None, "tm", "chan", None, "feed"),
        P(None, "tm", "feed", None, "chan", None, None, None),
        P(),
        P(None, "feed"),
        P(),
        P("tm", "chan"),
        P(),
    )
    out_specs = (P(None, "feed"), P())

    return jax.shard_map(shards, mesh=mesh, in_specs=in_specs, out_specs=out_specs, check_vma=False)
```

```python
import math

import jax
import jax.numpy as jnp
import numpy as np
from jax import lax
from jax.experimental import pallas as pl
from jax.experimental.pallas import tpu as pltpu
from jax.sharding import PartitionSpec as P

CYL = 16
NSF = 256
EWB = 32
NSB = 512
BANDS = 16
ROWS = 8
GROUPS = 4
BATCH = 4
FROM = 2
LANES = 128


full_turn = 2.0 * math.pi


def east_tables():
    angle = np.float32(full_turn / EWB) * (
        np.arange(EWB)[:, None] * np.arange(CYL)[None, :] % EWB
    ).astype(np.float32)
    real = np.cos(angle) / np.float32(math.sqrt(EWB))
    imag = -np.sin(angle) / np.float32(math.sqrt(EWB))
    parts = np.array([[real, -imag], [imag, real]], np.float32)
    same = np.eye(ROWS, dtype=np.float32)
    forward = np.einsum("abec,rs->arebcs", parts, same)
    forward = forward.reshape(2 * ROWS * EWB, 2 * CYL * ROWS)
    return jnp.asarray(forward, jnp.bfloat16), jnp.asarray(forward.T, jnp.bfloat16)


def north_parts():
    angle = np.float32(full_turn / NSB) * (
        np.arange(NSB)[:, None] * np.arange(NSF)[None, :] % NSB
    ).astype(np.float32)
    parts = np.stack([np.cos(angle), -np.sin(angle)]) / np.float32(math.sqrt(NSB))
    return jnp.asarray(parts, jnp.bfloat16)


def north_kernel(rows, parts, forward, adjoint):
    row = lax.broadcasted_iota(jnp.int32, (NSF, NSF), 0)
    chosen = jnp.where(row == rows[...], 1.0, 0.0)
    columns = chosen.astype(jnp.bfloat16)
    lines = chosen.T.astype(jnp.bfloat16)
    for part in range(2):
        table = parts[part]
        wide = jnp.dot(table, columns, preferred_element_type=jnp.float32)
        tall = lax.dot_general(
            lines, table, (((1,), (1,)), ((), ())), preferred_element_type=jnp.float32
        )
        same, swap = (lambda i: slice(i * NSB, (i + 1) * NSB)), (lambda i: slice(i * NSF, (i + 1) * NSF))
        for other in range(2):
            sign = -1.0 if part and other else 1.0
            m, n = same(part ^ other), swap(other)
            adjoint[m, n] = (sign * wide).astype(jnp.bfloat16)
            forward[n, m] = (sign * tall).astype(jnp.bfloat16)


def north_tables(rows):
    return pl.pallas_call(
        north_kernel,
        out_shape=[
            pltpu.VMEM((2 * NSF, 2 * NSB), jnp.bfloat16),
            pltpu.VMEM((2 * NSB, 2 * NSF), jnp.bfloat16),
        ],
        name="north",
    )(rows.reshape(1, NSF), north_parts())


def band_basis(chan_index, chans_total):
    term_index = jnp.arange(BANDS).astype(jnp.float32)
    return math.sqrt(2.0 / chans_total) * jnp.cos(
        math.pi * (chan_index[:, None] + 0.5) * term_index[None, :] / chans_total
    )


def sky_kernel(partners, cuts, span, chan_start, chans_total, volts, delay_ref, band_ref, *refs):
    outs, (delays, band_phase, held, order, small, arrived) = refs[:-6], refs[-6:]
    _, _, times, chans, pols, width = held.shape
    me = lax.axis_index("feed")
    first_chan = lax.axis_index("chan") * volts.shape[2] + chan_start
    tables = [
        pltpu.make_async_copy(delay_ref, delays, small.at[0]),
        pltpu.make_async_copy(band_ref, band_phase, small.at[1]),
    ]
    for copy in tables:
        copy.start()
    copies = [
        pltpu.make_async_copy(
            volts.at[:, pl.ds((me ^ partner) * times, times), pl.ds(chan_start, chans)],
            held.at[index],
            arrived.at[index],
        )
        for index, partner in enumerate(partners)
    ]
    for copy in copies:
        copy.start()
    row = lax.broadcasted_iota(jnp.int32, (width, width), 0)
    column = lax.broadcasted_iota(jnp.int32, (width, width), 1)
    target = (row % CYL) * span + row // CYL
    order[...] = jnp.where(target == column, 1.0, 0.0).astype(jnp.bfloat16)
    term = lax.broadcasted_iota(jnp.int32, (1, BANDS), 1).astype(jnp.float32)
    for copy in tables:
        copy.wait()
    phases = []
    for chan in range(chans):
        place = (first_chan + chan).astype(jnp.float32)
        frequency = 0.4 + 0.4 * (place + 0.5) / chans_total
        basis = math.sqrt(2.0 / chans_total) * jnp.cos(
            math.pi * (place + 0.5) * term / chans_total
        )
        offset = jnp.sum(band_phase[...] * basis, 1, keepdims=True)
        phases.append(full_turn * frequency * delays[...] + offset)
    phases = jnp.concatenate(phases, 0)
    cosine, sine = jnp.cos(phases), -jnp.sin(phases)
    for index, partner in enumerate(partners):
        copies[index].wait()
        for chan in range(chans):
            block = held[index, :, :, chan].astype(jnp.float32)
            for pol in range(pols):
                unit = chan * pols + pol
                real, imag = block[0, :, pol], block[1, :, pol]
                gr, gi = cosine[unit : unit + 1], sine[unit : unit + 1]
                both = jnp.concatenate([gr * real - gi * imag, gr * imag + gi * real], 0)
                both = jnp.dot(
                    both.astype(jnp.bfloat16), order[...], preferred_element_type=jnp.float32
                )
                shift = partner * span % LANES
                if shift:
                    both = jnp.concatenate(
                        [
                            pltpu.roll(both[:, at : at + LANES], shift, 1)
                            for at in range(0, width, LANES)
                        ],
                        1,
                    )
                both = both.astype(jnp.bfloat16)
                piece = sum(unit >= cut for cut in cuts[1:-1])
                out = outs[index * (len(cuts) - 1) + piece]
                out[0, unit - cuts[piece]] = both[:times]
                out[1, unit - cuts[piece]] = both[times:]


def sky_blocks(voltages, delays, band_phase, peers, partners, part, cuts, chans_total):
    _, times, chans, pols, width = voltages.shape
    block = times // peers
    half = chans // 2
    outs = [
        jax.ShapeDtypeStruct((2, high - low, block, width), jnp.bfloat16)
        for _ in partners
        for low, high in zip(cuts[:-1], cuts[1:])
    ]
    result = pl.pallas_call(
        lambda *refs: sky_kernel(partners, cuts, width // CYL, part * half, chans_total, *refs),
        in_specs=[pl.BlockSpec(memory_space=pl.ANY)] * 3,
        out_specs=[pl.BlockSpec(memory_space=pltpu.VMEM)] * len(outs),
        scratch_shapes=[
            pltpu.VMEM(delays.shape, delays.dtype),
            pltpu.VMEM(band_phase.shape, band_phase.dtype),
            pltpu.VMEM((len(partners), 2, block, half, pols, width), jnp.bfloat16),
            pltpu.VMEM((width, width), jnp.bfloat16),
            pltpu.SemaphoreType.DMA((2,)),
            pltpu.SemaphoreType.DMA((len(partners),)),
        ],
        out_shape=outs,
        compiler_params=pltpu.CompilerParams(vmem_limit_bytes=48 << 20),
        name="sky",
    )(voltages, delays, band_phase)
    pieces = len(cuts) - 1
    return [result[i * pieces : (i + 1) * pieces] for i in range(len(partners))]


def group_sky(group, blocks):
    peers, width = len(blocks), blocks[0].shape[-1]
    span = width // CYL
    per_tile = LANES // span
    times = slice(group * ROWS, (group + 1) * ROWS)
    lane = lax.broadcasted_iota(jnp.int32, (ROWS, LANES), 1) // span
    pieces = []
    for part in range(2):
        loaded = [blocks[k][part, 0, times].astype(jnp.float32) for k in range(peers)]
        for c in range(CYL):
            tile, turn = divmod(c, per_tile)
            at = tile * LANES
            for half in range(NSF // LANES):
                value = None
                for slot in range(per_tile):
                    piece = loaded[half * per_tile + slot][:, at : at + LANES]
                    spot = (turn + slot) % per_tile
                    value = piece if value is None else jnp.where(lane == spot, piece, value)
                if turn:
                    value = pltpu.roll(value, LANES - turn * span, 1)
                pieces.append(value)
    return jnp.concatenate(
        [jnp.concatenate(pieces[i : i + 2], 1) for i in range(0, len(pieces), 2)], 0
    )


def batch_torque(groups, blocks, ref_beams, keep, weight, east_fwd, east_adj, north_fwd, north_adj):
    half = ROWS * EWB
    span = slice(groups[0] * ROWS, (groups[-1] + 1) * ROWS)
    skies, easts = [], []
    for group in groups:
        sky = group_sky(group, blocks).astype(jnp.bfloat16)
        east = jnp.dot(east_fwd[...], sky, preferred_element_type=jnp.float32)
        east = east.astype(jnp.bfloat16)
        skies.append(sky)
        easts.append(jnp.concatenate([east[:half], east[half:]], 1))
    beams = jnp.dot(
        jnp.concatenate(easts, 0), north_fwd[...], preferred_element_type=jnp.float32
    ).reshape(len(groups) * ROWS, EWB, 2 * NSB)
    residual = jnp.concatenate(
        [
            (
                (beams[:, :, part * NSB : (part + 1) * NSB] - ref_beams(part, span).astype(jnp.float32))
                * weight[...][None]
            ).astype(jnp.bfloat16)
            for part in range(2)
        ],
        2,
    ).reshape(len(groups) * half, 2 * NSB)
    backs = jnp.dot(residual, north_adj[...], preferred_element_type=jnp.float32)
    backs = backs.astype(jnp.bfloat16)
    rows = CYL * ROWS
    total = 0.0
    for at, group in enumerate(groups):
        back = backs[at * half : (at + 1) * half]
        back = jnp.concatenate([back[:, :NSF], back[:, NSF:]], 0)
        field = jnp.dot(east_adj[...], back, preferred_element_type=jnp.float32)
        sky = skies[at].astype(jnp.float32)
        torque = field[:rows] * sky[rows:] - field[rows:] * sky[:rows]
        kept = keep[0, group * ROWS : (group + 1) * ROWS][None, :, :1]
        total += jnp.sum(torque.reshape(CYL, ROWS, NSF) * kept, 1)
    return total


def pack(sums, shares, slots, peers, others, span):
    per_tile = LANES // span
    rows = CYL // per_tile
    me = lax.axis_index("feed")
    lane = lax.broadcasted_iota(jnp.int32, (rows, LANES), 1) // span
    band = sum(
        shares[unit : unit + 1] * jnp.sum(sums[1][unit], keepdims=True)
        for unit in range(sums[1].shape[0])
    )
    for partner in range(peers):
        half, slot = divmod(partner, per_tile)
        block = []
        for pol in range(sums[0].shape[0]):
            tile = sums[0][pol][:, half * LANES : (half + 1) * LANES]
            value = None
            for spot in range(per_tile):
                shift = (spot - slot) * span % LANES
                piece = pltpu.roll(tile, shift, 1) if shift else tile
                piece = piece[spot * rows : (spot + 1) * rows]
                value = piece if value is None else jnp.where(lane == spot, piece, value)
            block.append(value)
        lines = [value[row : row + 1] for value in block for row in range(rows)] + [band]
        for other in range(others):
            for at, line in enumerate(lines):
                slots[(me ^ partner) * others + other, :, at * LANES : (at + 1) * LANES] = line


def unpack_kernel(slots, delay_grad, band_grad):
    pols, width = delay_grad.shape
    span = width // CYL
    rows = CYL * span // LANES
    total = slots[0]
    for other in range(1, slots.shape[0]):
        total += slots[other]
    parts, rest = [], total
    for _ in range(3):
        parts.append(rest.astype(jnp.bfloat16).astype(jnp.float32))
        rest = rest - parts[-1]
    lane = lax.broadcasted_iota(jnp.int32, (LANES, width), 0)
    feed = lax.broadcasted_iota(jnp.int32, (LANES, width), 1)
    where = (lane % span) * CYL + (lane // span) * rows
    moved = 0.0
    for row in range(rows):
        chosen = jnp.where(where + row == feed, 1.0, 0.0).astype(jnp.bfloat16)
        lines = jnp.concatenate(
            [
                part[:, (pol * rows + row) * LANES : (pol * rows + row + 1) * LANES]
                for pol in range(pols)
                for part in parts
            ],
            0,
        )
        moved += jnp.dot(lines.astype(jnp.bfloat16), chosen, preferred_element_type=jnp.float32)
    for pol in range(pols):
        first, second, third = (moved[pol * 3 + i : pol * 3 + i + 1] for i in range(3))
        delay_grad[pol : pol + 1] = first + (second + third)
        band = total[:, pols * rows * LANES :]
        shift = -pol * BANDS % LANES
        band = pltpu.roll(band, shift, 1) if shift else band
        band_grad[pol : pol + 1] = band[:, :BANDS]


def beam_kernel(peers, groups, low, pack_for, *refs):
    ref_beams, keep, weight, scales, shares = refs[peers : peers + 5]
    outs = 3 if pack_for else 2

    def read(part, span):
        if len(ref_beams.shape) == 6:
            return ref_beams[part, span, 0, 0]
        return ref_beams[pl.program_id(0), part, span]

    before, out = refs[peers + 9 : -outs], refs[-outs:]
    torque = sum(
        batch_torque(
            range(first, min(first + BATCH, groups)),
            refs[:peers],
            read,
            keep,
            weight,
            *refs[peers + 5 : peers + 9],
        )
        for first in range(0, groups, BATCH)
    )
    unit, step = pl.program_id(0), pl.program_id(1)

    @pl.when((unit == 0) & (step == 0))
    def _():
        for new, old in zip(out, before):
            new[...] = old[...]
        if not before:
            for new in out[:2]:
                new[...] = jnp.zeros_like(new)

    unit = unit + low
    out[0][unit % out[0].shape[0]] += torque * scales[unit]
    out[1][unit] += jnp.sum(torque, 0, keepdims=True)
    if pack_for:

        @pl.when((unit - low == pl.num_programs(0) - 1) & (step == pl.num_programs(1) - 1))
        def _():
            pack(out, shares, out[2], peers, pack_for, refs[0].shape[-1] // CYL)


def hold_refs(ref_beams, chunks):
    _, times, _, pols, _, _ = ref_beams.shape

    def kernel(source, *refs):
        outs, arrived = refs[:-1], refs[-1]
        copies = [
            pltpu.make_async_copy(
                source.at[:, :, unit // pols, unit % pols], out.at[unit - low], arrived.at[unit - chunks[0][0]]
            )
            for out, (low, high) in zip(outs, chunks)
            for unit in range(low, high)
        ]
        for copy in copies:
            copy.start()
        for copy in copies:
            copy.wait()

    return pl.pallas_call(
        kernel,
        in_specs=[pl.BlockSpec(memory_space=pl.ANY)],
        out_specs=[pl.BlockSpec(memory_space=pltpu.VMEM)] * len(chunks),
        out_shape=[
            pltpu.VMEM((high - low, 2, times, EWB, NSB), jnp.bfloat16) for low, high in chunks
        ],
        scratch_shapes=[pltpu.SemaphoreType.DMA((chunks[-1][1] - chunks[0][0],))],
        compiler_params=pltpu.CompilerParams(vmem_limit_bytes=4 << 20),
        name="hold",
    )(ref_beams)


def unit_torque(blocks, offsets, ref_beams, keep, weight, scales, shares, tables, low, high, before, pack_for, shape):
    peers = len(blocks)
    block_times, width = blocks[0].shape[2:]
    chans, pols = shape
    sums = ((pols, CYL, NSF), (chans * pols, 1, NSF))
    if pack_for:
        sums += ((peers * pack_for, 1, pols * width + LANES),)
    whole = lambda shape: pl.BlockSpec(
        shape, lambda u, g: (0,) * len(shape), pipeline_mode=pl.Buffered(1)
    )
    unit = lambda offset: (lambda u, g: (0, u + offset, g, 0))
    groups = min(GROUPS, block_times // ROWS)
    times = groups * ROWS
    return pl.pallas_call(
        lambda *refs: beam_kernel(peers, groups, low, pack_for, *refs),
        grid=(high - low, block_times // times),
        in_specs=[pl.BlockSpec((2, 1, times, width), unit(offset)) for offset in offsets]
        + [
            pl.BlockSpec(memory_space=pltpu.VMEM)
            if len(ref_beams.shape) == 5
            else pl.BlockSpec(
                (2, times, 1, 1, EWB, NSB),
                lambda u, g: (0, g, (u + low) // pols, (u + low) % pols, 0, 0),
            ),
            pl.BlockSpec((1, times, LANES), lambda u, g: ((u + low) // pols, g, 0)),
            whole(weight.shape),
            pl.BlockSpec(memory_space=pltpu.SMEM),
            whole(shares.shape),
        ]
        + [whole(t.shape) for t in tables]
        + [whole(b.shape) for b in before],
        out_specs=[pl.BlockSpec(s, lambda u, g: (0, 0, 0)) for s in sums],
        out_shape=[jax.ShapeDtypeStruct(s, jnp.float32) for s in sums],
        compiler_params=pltpu.CompilerParams(vmem_limit_bytes=32 << 20),
        name="beams",
    )(*blocks, ref_beams, keep, weight, scales, shares, *tables, *before)


def shards(voltages, beam_refs, beam_weight, delays, band_phase, rfi_flags, grid_rows):
    _, local_times, local_chans, pol_count, width = voltages.shape
    peers = lax.axis_size("feed")
    me = lax.axis_index("feed")
    others = lax.axis_size("chan") * lax.axis_size("tm")
    times_total = local_times * lax.axis_size("tm")
    chans_total = local_chans * lax.axis_size("chan")
    block_times = local_times // peers
    partners = me ^ jnp.arange(peers, dtype=jnp.int32)
    chan_index = (
        lax.axis_index("chan") * local_chans + jnp.arange(local_chans, dtype=jnp.int32)
    ).astype(jnp.float32)
    frequency = 0.4 + 0.4 * (chan_index + 0.5) / chans_total
    basis = band_basis(chan_index, chans_total)
    voltages, delays, band_phase = (
        pltpu.with_memory_space_constraint(a, pltpu.HBM) for a in (voltages, delays, band_phase)
    )

    units = local_chans * pol_count
    middle = units // 2
    ends = [0, middle, units - 2, units - 1, units]
    chunks = list(zip(ends[:-1], ends[1:]))
    blocks = [[None] * peers for _ in chunks]
    offsets = [[0] * peers for _ in chunks]

    made = {}
    for kind, group, part, piece in issue_plan(peers):
        mine = [i for i, (low, _) in enumerate(chunks) if (low >= middle) == part]
        remote = group[0] >= peers // 2
        cuts = [chunks[i][0] - part * middle for i in mine] + [middle]
        if kind == "sky":
            cuts = cuts if remote else [0, middle]
            blocks_made = sky_blocks(
                voltages, delays, band_phase, peers, group, part, cuts, chans_total
            )
            for partner, pieces in zip(group, blocks_made):
                made[partner, part] = pieces
            continue
        partner = group[0]
        block = made[partner, part][piece]
        if partner:
            pairs = [(i, i ^ partner) for i in range(peers)]
            block = lax.ppermute(block, "feed", pairs)
        for at, i in enumerate(mine):
            if at == piece or not remote:
                blocks[i][partner] = block
                offsets[i][partner] = 0 if remote else cuts[at]

    rows = grid_rows.reshape(peers, -1)[partners].reshape(-1)
    north_fwd, north_adj = north_tables(rows)
    east_fwd, east_adj = east_tables()
    tables = (east_fwd, east_adj, north_fwd, north_adj)
    flags = lax.dynamic_slice_in_dim(rfi_flags, me * block_times, block_times, 0)
    keep = (1 - flags).astype(jnp.float32).T
    keep = jnp.broadcast_to(keep[:, :, None], (local_chans, block_times, LANES))
    ref_beams = beam_refs.reshape(2, block_times, local_chans, pol_count, EWB, NSB)
    ref_beams = pltpu.with_memory_space_constraint(ref_beams, pltpu.HBM)
    scales = jnp.repeat(full_turn * frequency, pol_count) / times_total
    shares = basis[:, None, None, :] * jnp.eye(pol_count)[None, :, :, None] / times_total
    shares = shares.reshape(units, pol_count * BANDS)
    shares = jnp.pad(shares, ((0, 0), (0, LANES - shares.shape[1])))
    late = ()
    if block_times <= GROUPS * ROWS:
        late = hold_refs(ref_beams, chunks[FROM:])
    sums = ()
    for i, (low, high) in enumerate(chunks):
        pack_for = others if i == len(chunks) - 1 else 0
        held = late[i - FROM] if i >= FROM and late else ref_beams
        sums = unit_torque(
            blocks[i],
            offsets[i],
            held,
            keep,
            beam_weight,
            scales,
            shares,
            tables,
            low,
            high,
            sums,
            pack_for,
            (local_chans, pol_count),
        )
    slots = lax.all_to_all(sums[2], ("feed", "chan", "tm"), 0, 0, tiled=True)
    return pl.pallas_call(
        unpack_kernel,
        out_shape=(
            jax.ShapeDtypeStruct((pol_count, width), jnp.float32),
            jax.ShapeDtypeStruct((pol_count, BANDS), jnp.float32),
        ),
        name="unpack",
    )(slots)


def halves(peers):
    return list(range(peers - 1, peers // 2, -2)) + list(range(peers - 2, peers // 2 - 1, -2)), list(range(1, peers // 2))


def issue_plan(peers):
    far, near = halves(peers)
    send = lambda group, part, piece=0: [("send", [partner], part, piece) for partner in group]
    return (
        [("sky", far[:1], 0, 0)]
        + send(far[:1], 0)
        + [("sky", far[1:], 0, 0)]
        + send(far[1:], 0)
        + [("sky", near + [0], 0, 0)]
        + send(near + [0], 0)
        + [("sky", near + [0], 1, 0)]
        + send(near + [0], 1)
        + [("sky", far, 1, 0)]
        + send(far, 1)
        + send(far, 1, 1)
        + send(far, 1, 2)
    )


def solution(mesh):
    in_specs = (
        P(None, "tm", "chan", None, "feed"),
        P(None, "tm", "feed", None, "chan", None, None, None),
        P(),
        P(None, "feed"),
        P(),
        P("tm", "chan"),
        P(),
    )
    out_specs = (P(None, "feed"), P())

    return jax.shard_map(shards, mesh=mesh, in_specs=in_specs, out_specs=out_specs, check_vma=False)
```
